32 devices in a mesh: dom: 16 (over z, y, core), rep: 2 (over x).
Axes of the slice: x: 2, y: 2, z: 4, core: 2. Of those that a mesh axis runs over, the one named last changes fastest.
Arguments:
- features: bfloat16 [4096, 1024], P('dom'), may hold values from -6 to 6
- tiles: bfloat16 [2, 32, 12, 128, 128], P(None, 'dom'), may hold values from 0 to 2, as said below
- columns: int32 [2, 32, 12], P(None, 'dom'), may hold values from 0 to 31, as said below
- counts: int32 [2, 32], P(None, 'dom'), may hold values from 1 to 12, as said below
- degrees: int32 [2, 4096], P(None, 'dom'), may hold values from 16 to 64
- w_self: bfloat16 [1024, 1024], replicated, may hold values from -0.1875 to 0.1875
- w_in: bfloat16 [1024, 1024], replicated, may hold values from -1 to 1
- w_out: bfloat16 [1024, 1024], replicated, may hold values from -1 to 1
Outputs:
- layer_out: bfloat16 [4096, 1024], P('dom')
The draws below stay inside these ranges and needn't reach their ends.
Inputs may be any that keep to these rules, and one draw needn't show every extreme that they name: Within one block-row the 12 block-columns are distinct; only the first counts slots are read. `counts`: in each relation some block-row has all 12 slots live. `tiles`: edge weights are zero or positive.
All inputs are finite; a program needn't handle non-finite values.
Results may differ from the reference program's by a relative error of at most 0.0038.
Values may be sent and summed in bfloat16 or wider, within the bound.
No kernel may reach another device: no remote copies, remote signals or barrier semaphores. Data moves between devices by JAX's collectives and lax.ppermute only.
A program may use at most 64 MiB of HBM per device.

```python
import jax
import jax.numpy as jnp
from jax import lax

H = 1024
TB = 128
BLOCK_ROWS = 32
NODES = 4096
SLOTS = 12


def draw_tiles(key, part):
    keep_key, value_key = jax.random.split(key, 2)
    shape = (2, BLOCK_ROWS, SLOTS, TB, TB)
    keep = jax.random.randint(keep_key, shape, 0, max(2, TB // 2)) == 0
    values = jax.random.uniform(value_key, shape, jnp.float32, 0.5, 1.5)
    return jnp.where(keep, values, jnp.float32(0.0)).astype(jnp.bfloat16)


def draw_columns(key, part):
    row_keys = jax.random.split(key, 2 * BLOCK_ROWS)
    orders = jax.vmap(lambda row_key: jax.random.permutation(row_key, BLOCK_ROWS))(row_keys)
    return orders[:, :SLOTS].reshape(2, BLOCK_ROWS, SLOTS).astype(jnp.int32)


def draw_counts(key, part):
    hub_key, base_key, force_key = jax.random.split(key, 3)
    hubs = jax.random.randint(hub_key, (2, BLOCK_ROWS), 0, 8) == 0
    lowest = max(1, SLOTS // 8)
    base = jax.random.randint(base_key, (2, BLOCK_ROWS), lowest, SLOTS // 2 + 1)
    forced = jax.random.randint(force_key, (2, 1), 0, BLOCK_ROWS)
    places = jnp.arange(BLOCK_ROWS, dtype=jnp.int32)[None, :]
    return jnp.where(hubs | (places == forced), SLOTS, base).astype(jnp.int32)


def touch_ends(entries, rng, low, largest):
    index_at = [jax.random.randint(jax.random.fold_in(rng, axis), (), 0, length) for axis, length in enumerate(entries.shape)]
    longest = entries.shape.index(max(entries.shape))
    next_to = index_at[:longest] + [(index_at[longest] + 1) % entries.shape[longest]] + index_at[longest + 1:]
    return entries.at[tuple(index_at)].set(low).at[tuple(next_to)].set(largest)


def levels(key, shape, shards, smallest, top_value):
    factor_of = 1.0
    for axis_at, shards_of in shards:
        steps = jax.random.uniform(jax.random.fold_in(jax.random.fold_in(key, 6), axis_at), (shards_of,), jnp.float32, smallest / len(shards), top_value / len(shards))
        factor_of = factor_of * jnp.repeat(jnp.exp(steps), shape[axis_at] // shards_of).reshape((-1,) + (1,) * (len(shape) - 1 - axis_at))
    return factor_of


def bell_draw(stream_key, dims, scale, limit, cuts=(), kind=jnp.bfloat16):
    values = jax.random.normal(stream_key, dims, jnp.float32) * scale
    if len(cuts) > 0:
        values = levels(stream_key, dims, cuts, -0.22, 0.18) * values
    return jnp.clip(values, min=-limit, max=limit).astype(kind)


def setup_inputs(seed: int = 0) -> dict:
    key_of = jax.random.split(jax.random.key(seed), 9)
    features = bell_draw(key_of[0], (NODES, H), 1.0, 6.0, ((0, 16),))
    tiles = draw_tiles(jax.random.fold_in(key_of[8], 71), 0)
    columns = draw_columns(jax.random.fold_in(key_of[8], 71), 0)
    counts = draw_counts(jax.random.fold_in(key_of[8], 71), 0)
    degrees = touch_ends(jax.random.randint(key_of[4], (2, NODES), 16, 65), jax.random.fold_in(key_of[4], 1), 16, 64).astype(jnp.int32)
    w_self = bell_draw(key_of[5], (H, H), H ** -0.5, 0.1875)
    w_in = bell_draw(key_of[6], (H, H), (H // 32) ** -0.5, 1.0)
    w_out = bell_draw(key_of[7], (H, H), (H // 32) ** -0.5, 1.0)
    return {"features": features, "tiles": tiles, "columns": columns, "counts": counts, "degrees": degrees, "w_self": w_self, "w_in": w_in, "w_out": w_out}


def relation_sum(features, rel_tiles, rel_columns, rel_counts):
    blocks = features.reshape(BLOCK_ROWS, TB, H)
    slot_ids = jnp.arange(SLOTS, dtype=jnp.int32)

    def one_row(carry, item):
        row_tiles, row_columns, row_count = item
        live_slots = (slot_ids < row_count).astype(jnp.float32)
        picked = blocks[row_columns.astype(jnp.int32)].astype(jnp.float32)
        weighted = row_tiles.astype(jnp.float32) * live_slots[:, None, None]
        return carry, jnp.einsum("kij,kjh->ih", weighted, picked)

    unused, sums = lax.scan(one_row, jnp.float32(0.0), (rel_tiles, rel_columns, rel_counts))
    return sums.reshape(NODES, H)


def reference(features, tiles, columns, counts, degrees, w_self, w_in, w_out):
    summed_in = relation_sum(features, tiles[0], columns[0], counts[0])
    summed_out = relation_sum(features, tiles[1], columns[1], counts[1])
    agg_in = (summed_in / degrees[0][:, None].astype(jnp.float32)).astype(jnp.bfloat16)
    agg_out = (summed_out / degrees[1][:, None].astype(jnp.float32)).astype(jnp.bfloat16)
    hidden = jnp.dot(features, w_self, preferred_element_type=jnp.float32)
    hidden = hidden + jnp.dot(agg_in, w_in, preferred_element_type=jnp.float32)
    hidden = hidden + jnp.dot(agg_out, w_out, preferred_element_type=jnp.float32)
    return jax.nn.relu(hidden).astype(jnp.bfloat16)
```

```python
import functools

import jax
import jax.numpy as jnp
from jax import lax
from jax.experimental import pallas as pl
from jax.experimental.pallas import tpu as pltpu
from jax.sharding import PartitionSpec as P

F32 = jnp.float32
BF16 = jnp.bfloat16


def chip_ring(chips):
    half = chips // 2
    return [2 * o for o in range(half)] + [2 * o + 1 for o in reversed(range(half))]


def ring_route(devices, distance):
    ring = chip_ring(devices // 2)
    size = len(ring)
    route = []
    for place, chip in enumerate(ring):
        target = ring[(place + distance) % size]
        route += [(2 * chip + core, 2 * target + core) for core in range(2)]
    return sorted(route)


def core_route(devices):
    return [(d, d ^ 1) for d in range(devices)]


def chip_at(place, chips):
    place = lax.rem(place + 2 * chips, chips)
    return jnp.where(place < chips // 2, 2 * place, 2 * (chips - 1 - place) + 1)


def place_of(chip, chips):
    side = lax.rem(chip, 2)
    rung = chip // 2
    return jnp.where(side == 0, rung, chips - 1 - rung)


def gather_ring(own, sibling, devices):
    chips = devices // 2
    ahead, behind = ring_route(devices, 1), ring_route(devices, -1)
    pieces = [(own, 0, 0), (sibling, 0, 1)]
    forward = [own, sibling]
    backward = [own, sibling]
    for step in range(1, (chips - 1) // 2 + 1):
        forward[0] = lax.ppermute(forward[0], "dom", ahead)
        backward[0] = lax.ppermute(backward[0], "dom", behind)
        forward[1] = lax.ppermute(forward[1], "dom", ahead)
        backward[1] = lax.ppermute(backward[1], "dom", behind)
        pieces += [(forward[0], -step, 0), (backward[0], step, 0)]
        pieces += [(forward[1], -step, 1), (backward[1], step, 1)]
    if chips % 2 == 0:
        far = chips // 2
        pieces.append((lax.ppermute(forward[0], "dom", ahead), far, 0))
        pieces.append((lax.ppermute(backward[1], "dom", behind), far, 1))
    return pieces


def aggregate_body(origins, slots, chips, *refs):
    count = len(origins)
    columns_own, columns_sib = refs[:2]
    tiles_own, tiles_sib, degrees_own, degrees_sib = refs[2:6]
    piece_refs = refs[6 : 6 + count]
    out_own, out_sib, blocks = refs[6 + count :]
    rows = piece_refs[0].shape[0]
    width = piece_refs[0].shape[1]
    tile = tiles_own.shape[-1]
    position = lax.axis_index("dom")
    core = lax.rem(position, 2)
    place = place_of(position // 2, chips)
    for ref, (offset, other) in zip(piece_refs, origins):
        chip = chip_at(place + offset, chips)
        source = 2 * chip + (1 - core if other else core)
        blocks[pl.ds(pl.multiple_of(source * rows, rows), rows), :] = ref[...]
    local = rows // tile
    for columns, tiles, degrees, out in (
        (columns_own, tiles_own, degrees_own, out_own),
        (columns_sib, tiles_sib, degrees_sib, out_sib),
    ):
        for relation in range(2):
            for row in range(local):
                live_count = columns[relation, row, slots]

                def one(slot, total):
                    live = slot < live_count
                    column = jnp.where(live, columns[relation, row, slot], 0)
                    weights = tiles[relation, row, slot]
                    weights = jnp.where(live, weights, jnp.zeros_like(weights))
                    panel = blocks[pl.ds(pl.multiple_of(column * tile, tile), tile), :]
                    return total + jnp.dot(weights, panel, preferred_element_type=F32)

                total = lax.fori_loop(0, slots, one, jnp.zeros((tile, width), F32), unroll=12)
                degree = degrees[relation : relation + 1, row * tile : (row + 1) * tile].astype(F32)
                degree = jnp.broadcast_to(degree, (tile, tile)).T
                span = slice(row * tile, (row + 1) * tile)
                for start in range(0, width, tile):
                    part = total[:, start : start + tile] / degree
                    out[relation, span, start : start + tile] = part.astype(BF16)


def aggregate(pieces, columns, tiles, degrees, devices):
    rows, width = pieces[0][0].shape
    slots = tiles[0].shape[2]
    origins = tuple((offset, other) for _, offset, other in pieces)
    smem = pl.BlockSpec(memory_space=pltpu.SMEM)
    vmem = pl.BlockSpec(memory_space=pltpu.VMEM)
    out = jax.ShapeDtypeStruct((2, rows, width), BF16)
    return pl.pallas_call(
        functools.partial(aggregate_body, origins, slots, devices // 2),
        out_shape=[out, out],
        in_specs=[smem] * 2 + [vmem] * (4 + len(pieces)),
        out_specs=[vmem] * 2,
        scratch_shapes=[pltpu.VMEM((devices * rows, width), BF16)],
        compiler_params=pltpu.CompilerParams(vmem_limit_bytes=48 * 2**20),
        name="aggregate",
    )(*columns, *tiles, *degrees, *[piece for piece, _, _ in pieces])


def project_body(base, own, core_side, twin, diagonal, w_in, w_out, out):
    rep = lax.axis_index("rep")
    core = lax.rem(lax.axis_index("dom"), 2)
    width = own.shape[2]
    total = base[...]
    for part, quarter in (
        (own, 2 * rep + core),
        (core_side, 2 * rep + 1 - core),
        (twin, 2 * (1 - rep) + core),
        (diagonal, 2 * (1 - rep) + 1 - core),
    ):
        span = pl.ds(pl.multiple_of(quarter * width, width), width)
        total = total + jnp.dot(part[0], w_in[span, :], preferred_element_type=F32)
        total = total + jnp.dot(part[1], w_out[span, :], preferred_element_type=F32)
    out[...] = jnp.maximum(total, 0.0).astype(BF16)


def project(base, parts, w_in, w_out):
    vmem = pl.BlockSpec(memory_space=pltpu.VMEM)
    return pl.pallas_call(
        project_body,
        out_shape=jax.ShapeDtypeStruct(base.shape, BF16),
        in_specs=[vmem] * 7,
        out_specs=vmem,
        compiler_params=pltpu.CompilerParams(vmem_limit_bytes=32 * 2**20),
        name="project",
    )(base, *parts, w_in, w_out)


def on_device(features, tiles, columns, counts, degrees, w_self, w_in, w_out):
    devices = lax.axis_size("dom")
    reps = lax.axis_size("rep")
    position = lax.axis_index("dom")
    rep = lax.axis_index("rep")
    core = lax.rem(position, 2)
    width = features.shape[1] // (2 * reps)
    cores = core_route(devices)

    mine = lax.dynamic_slice_in_dim(features, (2 * rep + core) * width, width, 1)
    theirs = lax.dynamic_slice_in_dim(features, (2 * rep + 1 - core) * width, width, 1)
    sibling = lax.ppermute(theirs, "dom", cores)
    pieces = gather_ring(mine, sibling, devices)

    table = jnp.concatenate([columns, counts[:, :, None]], axis=2)
    table_sib = lax.ppermute(table, "dom", cores)
    tiles_sib = lax.ppermute(tiles, "dom", cores)
    degrees_sib = lax.ppermute(degrees, "dom", cores)
    base = jnp.dot(features, w_self, preferred_element_type=F32)

    own, other = aggregate(
        pieces, (table, table_sib), (tiles, tiles_sib), (degrees, degrees_sib), devices
    )
    core_side = lax.ppermute(other, "dom", cores)
    twin = lax.ppermute(own, "rep", [(r, (r + 1) % reps) for r in range(reps)])
    across = [
        (d * reps + r, (d ^ 1) * reps + (r + 1) % reps) for d in range(devices) for r in range(reps)
    ]
    diagonal = lax.ppermute(other, ("dom", "rep"), across)
    return project(base, (own, core_side, twin, diagonal), w_in, w_out)


def solution(mesh):
    placed = (
        P("dom", None),
        P(None, "dom", None, None, None),
        P(None, "dom", None),
        P(None, "dom"),
        P(None, "dom"),
        P(),
        P(),
        P(),
    )
    return jax.shard_map(
        on_device, mesh=mesh, in_specs=placed, out_specs=P("dom", None), check_vma=False
    )
```

```python
import functools

import jax
import jax.numpy as jnp
from jax import lax
from jax.experimental import pallas as pl
from jax.experimental.pallas import tpu as pltpu
from jax.sharding import PartitionSpec as P

F32 = jnp.float32
BF16 = jnp.bfloat16
SMEM = pl.BlockSpec(memory_space=pltpu.SMEM)
VMEM = pl.BlockSpec(memory_space=pltpu.VMEM)
HBM = pl.BlockSpec(memory_space=pltpu.HBM)


def params(mib):
    return pltpu.CompilerParams(vmem_limit_bytes=mib * 2**20)


def chip_ring(chips):
    half = chips // 2
    return [2 * o for o in range(half)] + [2 * o + 1 for o in reversed(range(half))]


def ring_route(devices, distance):
    ring = chip_ring(devices // 2)
    size = len(ring)
    route = []
    for place, chip in enumerate(ring):
        target = ring[(place + distance) % size]
        route += [(2 * chip + core, 2 * target + core) for core in range(2)]
    return sorted(route)


def swapped(route):
    return [(source, target ^ 1) for source, target in route]


def core_route(devices):
    return [(d, d ^ 1) for d in range(devices)]


def chip_at(place, chips):
    place = lax.rem(place + 2 * chips, chips)
    return jnp.where(place < chips // 2, 2 * place, 2 * (chips - 1 - place) + 1)


def place_of(chip, chips):
    side = lax.rem(chip, 2)
    rung = chip // 2
    return jnp.where(side == 0, rung, chips - 1 - rung)


def source_device(offset, other, chips):
    position = lax.axis_index("dom")
    core = lax.rem(position, 2)
    chip = chip_at(place_of(position // 2, chips) + offset, chips)
    return 2 * chip + (1 - core if other else core)


def pack_body(blocks, features, tiles_in, columns_in, counts_in, degrees_in, *refs):
    mine, theirs, tiles, info, columns, counts, degrees, arrived = refs
    rep = lax.axis_index("rep")
    core = lax.rem(lax.axis_index("dom"), 2)
    width = mine.shape[1]

    def quarter(core_of):
        return features.at[:, pl.ds(pl.multiple_of((2 * rep + core_of) * width, width), width)]

    moves = (
        (columns_in, columns),
        (counts_in, counts),
        (degrees_in, degrees),
        (quarter(core), mine),
        (quarter(1 - core), theirs),
        (tiles_in, tiles),
    )
    copies = [
        pltpu.make_async_copy(source, target, arrived.at[index])
        for index, (source, target) in enumerate(moves)
    ]
    for copy in copies:
        copy.start()
    for copy in copies[:3]:
        copy.wait()
    info[...] = jnp.full(info.shape, -1, jnp.int32)
    place = lax.broadcasted_iota(jnp.int32, (1, info.shape[1]), 1)
    _, local, slots = columns.shape
    for relation in range(2):
        for row in range(local):
            live = counts[relation, row]
            slot_of = jnp.full(place.shape, -1, jnp.int32)
            for slot in range(slots):
                target = jnp.where(slot < live, columns[relation, row, slot], -1)
                slot_of = jnp.where(place == target, slot, slot_of)
            index = relation * local + row
            info[index : index + 1, :] = slot_of
    info[2 * local : 2 * local + 2, 0 : degrees.shape[1]] = degrees[...]
    for copy in copies[3:]:
        copy.wait()


def pack(features, tiles, columns, counts, degrees, width, devices):
    rows = features.shape[0]
    blocks = devices * tiles.shape[1]
    piece = jax.ShapeDtypeStruct((rows, width), BF16)
    info = jax.ShapeDtypeStruct((8, max(rows, blocks)), jnp.int32)
    operands = [
        pltpu.with_memory_space_constraint(x, pltpu.HBM)
        for x in (features, tiles, columns, counts, degrees)
    ]
    return pl.pallas_call(
        functools.partial(pack_body, blocks),
        out_shape=[piece, piece, jax.ShapeDtypeStruct(tiles.shape, BF16), info],
        in_specs=[HBM] * 5,
        out_specs=[VMEM] * 4,
        scratch_shapes=[
            pltpu.SMEM(columns.shape, jnp.int32),
            pltpu.SMEM(counts.shape, jnp.int32),
            pltpu.VMEM(degrees.shape, jnp.int32),
            pltpu.SemaphoreType.DMA((6,)),
        ],
        compiler_params=params(24),
        name="pack",
    )(*operands)


def contribution(slot_of, tiles, relation, row, pieces, sources):
    local = tiles.shape[1]
    total = None
    for piece, source in zip(pieces, sources):
        weights = []
        for block in range(local):
            slot = slot_of[relation * local + row, source * local + block]
            one = tiles[relation, row, jnp.maximum(slot, 0)]
            weights.append(jnp.where(slot >= 0, one, jnp.zeros_like(one)))
        part = jnp.dot(
            jnp.concatenate(weights, axis=1), piece[...], preferred_element_type=F32
        )
        total = part if total is None else total + part
    return total


def absorb_body(origins, chips, seeded, *refs):
    slot_of, tiles = refs[0:2], refs[2:4]
    count = len(origins)
    pieces = refs[4 : 4 + count]
    seed = refs[4 + count] if seeded else None
    sums = refs[-1]
    tile = tiles[0].shape[-1]
    sources = [source_device(offset, other, chips) for offset, other in origins]
    for side in range(2):
        for relation in range(2):
            for row in range(tiles[side].shape[1]):
                span = slice(row * tile, (row + 1) * tile)
                part = contribution(slot_of[side], tiles[side], relation, row, pieces, sources)
                if seeded:
                    part = part + seed[side, relation, span, :]
                sums[side, relation, span, :] = part


def absorb(plan, pieces, sums, devices):
    infos, tiles = plan
    rows, width = pieces[0][0].shape
    origins = tuple((offset, other) for _, offset, other in pieces)
    seeds = [] if sums is None else [sums]
    return pl.pallas_call(
        functools.partial(absorb_body, origins, devices // 2, sums is not None),
        out_shape=jax.ShapeDtypeStruct((2, 2, rows, width), F32),
        in_specs=[SMEM] * 2 + [VMEM] * (2 + len(pieces) + len(seeds)),
        out_specs=VMEM,
        compiler_params=params(32),
        cost_estimate=pl.CostEstimate(
            flops=len(pieces) * 8 * rows * rows * width, bytes_accessed=0, transcendentals=0
        ),
        name="absorb",
    )(*infos, *tiles, *[piece for piece, _, _ in pieces], *seeds)


def close_body(origins, chips, side, slot_of, info, tiles, sums, *refs):
    pieces, out = refs[:-1], refs[-1]
    tile = tiles.shape[-1]
    local = tiles.shape[1]
    sources = [source_device(offset, other, chips) for offset, other in origins]
    for relation in range(2):
        for row in range(local):
            span = slice(row * tile, (row + 1) * tile)
            total = sums[side, relation, span, :]
            if pieces:
                total = total + contribution(slot_of, tiles, relation, row, pieces, sources)
            index = 2 * local + relation
            degree = info[index : index + 1, row * tile : (row + 1) * tile].astype(F32)
            degree = jnp.broadcast_to(degree, (tile, tile)).T
            for start in range(0, total.shape[1], tile):
                part = total[:, start : start + tile] / degree
                out[relation, span, start : start + tile] = part.astype(BF16)


def close(plan, pieces, sums, side, devices):
    infos, tiles = plan
    _, _, rows, width = sums.shape
    origins = tuple((offset, other) for _, offset, other in pieces)
    return pl.pallas_call(
        functools.partial(close_body, origins, devices // 2, side),
        out_shape=jax.ShapeDtypeStruct((2, rows, width), BF16),
        in_specs=[SMEM] + [VMEM] * (3 + len(pieces)),
        out_specs=VMEM,
        compiler_params=params(32),
        name="close",
    )(infos[side], infos[side], tiles[side], sums, *[piece for piece, _, _ in pieces])


def project_body(quarters, last, base, w_in, w_out, *refs):
    parts, out = refs[:-1], refs[-1]
    rep = lax.axis_index("rep")
    core = lax.rem(lax.axis_index("dom"), 2)
    total = base[...]
    for part, (far, other) in zip(parts, quarters):
        width = part.shape[2]
        quarter = 2 * (1 - rep if far else rep) + (1 - core if other else core)
        span = pl.ds(pl.multiple_of(quarter * width, width), width)
        total = total + jnp.dot(part[0], w_in[span, :], preferred_element_type=F32)
        total = total + jnp.dot(part[1], w_out[span, :], preferred_element_type=F32)
    out[...] = jnp.maximum(total, 0.0).astype(BF16) if last else total


def project(base, parts, quarters, w_in, w_out, last):
    return pl.pallas_call(
        functools.partial(project_body, quarters, last),
        out_shape=jax.ShapeDtypeStruct(base.shape, BF16 if last else F32),
        in_specs=[VMEM] * (3 + len(parts)),
        out_specs=VMEM,
        compiler_params=params(24),
        cost_estimate=pl.CostEstimate(
            flops=len(parts) * 2**28, bytes_accessed=0, transcendentals=0
        ),
        name="project",
    )(base, w_in, w_out, *parts)


def on_device(features, tiles, columns, counts, degrees, w_self, w_in, w_out):
    devices = lax.axis_size("dom")
    reps = lax.axis_size("rep")
    width = features.shape[1] // (2 * reps)
    chips = devices // 2
    cores = core_route(devices)
    ahead, behind = ring_route(devices, 1), ring_route(devices, -1)

    mine, theirs, tiles, info = pack(features, tiles, columns, counts, degrees, width, devices)

    forward = [mine, theirs]
    backward = [mine, theirs]
    steps = []
    for step in range(1, (chips - 1) // 2 + 1):
        found = []
        for other in range(2):
            swap = other == 1 and step == 1
            forward[other] = lax.ppermute(forward[other], "dom", swapped(ahead) if swap else ahead)
            backward[other] = lax.ppermute(backward[other], "dom", swapped(behind) if swap else behind)
            found += [(forward[other], -step, other), (backward[other], step, other)]
        steps.append(found)
    last = [
        (lax.ppermute(forward[0], "dom", ahead), chips // 2, 0),
        (lax.ppermute(backward[1], "dom", behind), chips // 2, 1),
    ]
    sibling = lax.ppermute(theirs, "dom", cores)
    plan = (
        (info, lax.ppermute(info, "dom", cores)),
        (tiles, lax.ppermute(tiles, "dom", cores)),
    )
    early = [(mine, 0, 0), (sibling, 0, 1)] + [piece for found in steps[:-1] for piece in found]
    sums = absorb(plan, early, None, devices)
    sums = absorb(plan, steps[-1], sums, devices)
    other = close(plan, last, sums, 1, devices)
    own = close(plan, last, sums, 0, devices)

    across = [
        (d * reps + r, (d ^ 1) * reps + (r + 1) % reps) for d in range(devices) for r in range(reps)
    ]
    diagonal = lax.ppermute(other, ("dom", "rep"), across)
    core_side = lax.ppermute(other, "dom", cores)
    twin = lax.ppermute(own, "rep", [(r, (r + 1) % reps) for r in range(reps)])

    hidden = jnp.dot(features, w_self, preferred_element_type=F32)
    hidden = project(hidden, (own, core_side), ((0, 0), (0, 1)), w_in, w_out, False)
    hidden = project(hidden, (diagonal,), ((1, 1),), w_in, w_out, False)
    return project(hidden, (twin,), ((1, 0),), w_in, w_out, True)


def solution(mesh):
    placed = (
        P("dom", None),
        P(None, "dom", None, None, None),
        P(None, "dom", None),
        P(None, "dom"),
        P(None, "dom"),
        P(),
        P(),
        P(),
    )
    return jax.shard_map(
        on_device, mesh=mesh, in_specs=placed, out_specs=P("dom", None), check_vma=False
    )
```

```python
import functools

import jax
import jax.numpy as jnp
from jax import lax
from jax.experimental import pallas as pl
from jax.experimental.pallas import tpu as pltpu
from jax.sharding import PartitionSpec as P

F32 = jnp.float32
BF16 = jnp.bfloat16
SMEM = pl.BlockSpec(memory_space=pltpu.SMEM)
VMEM = pl.BlockSpec(memory_space=pltpu.VMEM)
HBM = pl.BlockSpec(memory_space=pltpu.HBM)


def params(mib):
    return pltpu.CompilerParams(vmem_limit_bytes=mib * 2**20)


def chip_ring(chips):
    half = chips // 2
    return [2 * o for o in range(half)] + [2 * o + 1 for o in reversed(range(half))]


def ring_route(devices, distance):
    ring = chip_ring(devices // 2)
    size = len(ring)
    route = []
    for place, chip in enumerate(ring):
        target = ring[(place + distance) % size]
        route += [(2 * chip + core, 2 * target + core) for core in range(2)]
    return sorted(route)


def swapped(route):
    return [(source, target ^ 1) for source, target in route]


def core_route(devices):
    return [(d, d ^ 1) for d in range(devices)]


def place_of(chip, chips):
    side = lax.rem(chip, 2)
    rung = chip // 2
    return jnp.where(side == 0, rung, chips - 1 - rung)


def lane(offset, other, block, local):
    return (offset * 2 + other) * local + block


def pack_body(chips, features, tiles_in, columns_in, counts_in, degrees_in, *refs):
    mine, theirs, tiles, info, columns, counts, degrees, arrived = refs
    rep = lax.axis_index("rep")
    position = lax.axis_index("dom")
    core = lax.rem(position, 2)
    here = place_of(position // 2, chips)
    width = mine.shape[1]

    def quarter(core_of):
        return features.at[:, pl.ds(pl.multiple_of((2 * rep + core_of) * width, width), width)]

    moves = (
        (columns_in, columns),
        (counts_in, counts),
        (degrees_in, degrees),
        (quarter(core), mine),
        (quarter(1 - core), theirs),
        (tiles_in, tiles),
    )
    copies = [
        pltpu.make_async_copy(source, target, arrived.at[index])
        for index, (source, target) in enumerate(moves)
    ]
    for copy in copies:
        copy.start()
    for copy in copies[:3]:
        copy.wait()
    info[...] = jnp.full(info.shape, -1, jnp.int32)
    place = lax.broadcasted_iota(jnp.int32, (1, info.shape[1]), 1)
    _, local, slots = columns.shape
    for relation in range(2):
        for row in range(local):
            live = counts[relation, row]
            slot_of = jnp.full(place.shape, -1, jnp.int32)
            for slot in range(slots):
                column = columns[relation, row, slot]
                source = column // local
                offset = lax.rem(place_of(source // 2, chips) - here + chips, chips)
                other = lax.rem(lax.rem(source, 2) + core, 2)
                target = lane(offset, other, lax.rem(column, local), local)
                slot_of = jnp.where(place == jnp.where(slot < live, target, -1), slot, slot_of)
            index = relation * local + row
            info[index : index + 1, :] = slot_of
    info[2 * local : 2 * local + 2, 0 : degrees.shape[1]] = degrees[...]
    for copy in copies[3:]:
        copy.wait()


def pack(features, tiles, columns, counts, degrees, width, devices):
    rows = features.shape[0]
    blocks = devices * tiles.shape[1]
    piece = jax.ShapeDtypeStruct((rows, width), BF16)
    info = jax.ShapeDtypeStruct((8, max(rows, blocks)), jnp.int32)
    operands = [
        pltpu.with_memory_space_constraint(x, pltpu.HBM)
        for x in (features, tiles, columns, counts, degrees)
    ]
    return pl.pallas_call(
        functools.partial(pack_body, devices // 2),
        out_shape=[piece, piece, jax.ShapeDtypeStruct(tiles.shape, BF16), info],
        in_specs=[HBM] * 5,
        out_specs=[VMEM] * 4,
        scratch_shapes=[
            pltpu.SMEM(columns.shape, jnp.int32),
            pltpu.SMEM(counts.shape, jnp.int32),
            pltpu.VMEM(degrees.shape, jnp.int32),
            pltpu.SemaphoreType.DMA((6,)),
        ],
        compiler_params=params(24),
        name="pack",
    )(*operands)


def contribution(info, tiles, relation, row, side, pieces, origins, chips):
    local = tiles.shape[1]
    index = relation * local + row
    slots = info[index : index + 1, :]
    total = None
    for piece, (offset, other) in zip(pieces, origins):
        weights = []
        for block in range(local):
            at = lane(offset % chips, other ^ side, block, local)
            slot = slots[0, at]
            one = tiles[relation, row, jnp.maximum(slot, 0)]
            weights.append(jnp.where(slot >= 0, one, jnp.zeros_like(one)))
        part = jnp.dot(
            jnp.concatenate(weights, axis=1), piece[...], preferred_element_type=F32
        )
        total = part if total is None else total + part
    return total


def absorb_body(origins, chips, seeded, *refs):
    infos, tiles = refs[0:2], refs[2:4]
    count = len(origins)
    pieces = refs[4 : 4 + count]
    seed = refs[4 + count] if seeded else None
    sums = refs[-1]
    tile = tiles[0].shape[-1]
    for side in range(2):
        for relation in range(2):
            for row in range(tiles[side].shape[1]):
                span = slice(row * tile, (row + 1) * tile)
                part = contribution(
                    infos[side], tiles[side], relation, row, side, pieces, origins, chips
                )
                if seeded:
                    part = part + seed[side, relation, span, :]
                sums[side, relation, span, :] = part


def absorb(plan, pieces, sums, devices):
    infos, tiles = plan
    rows, width = pieces[0][0].shape
    origins = tuple((offset, other) for _, offset, other in pieces)
    seeds = [] if sums is None else [sums]
    return pl.pallas_call(
        functools.partial(absorb_body, origins, devices // 2, sums is not None),
        out_shape=jax.ShapeDtypeStruct((2, 2, rows, width), F32),
        in_specs=[VMEM] * (4 + len(pieces) + len(seeds)),
        out_specs=VMEM,
        compiler_params=params(32),
        cost_estimate=pl.CostEstimate(
            flops=len(pieces) * 8 * rows * rows * width, bytes_accessed=0, transcendentals=0
        ),
        name="absorb",
    )(*infos, *tiles, *[piece for piece, _, _ in pieces], *seeds)


def close_body(origins, chips, side, info, tiles, sums, *refs):
    pieces, out = refs[:-1], refs[-1]
    tile = tiles.shape[-1]
    local = tiles.shape[1]
    for relation in range(2):
        for row in range(local):
            span = slice(row * tile, (row + 1) * tile)
            total = sums[side, relation, span, :]
            total = total + contribution(
                info, tiles, relation, row, side, pieces, origins, chips
            )
            index = 2 * local + relation
            degree = info[index : index + 1, span].astype(F32)
            degree = jnp.broadcast_to(degree, (tile, tile)).T
            for start in range(0, total.shape[1], tile):
                part = total[:, start : start + tile] / degree
                out[relation, span, start : start + tile] = part.astype(BF16)


def close(plan, pieces, sums, side, devices):
    infos, tiles = plan
    _, _, rows, width = sums.shape
    origins = tuple((offset, other) for _, offset, other in pieces)
    return pl.pallas_call(
        functools.partial(close_body, origins, devices // 2, side),
        out_shape=jax.ShapeDtypeStruct((2, rows, width), BF16),
        in_specs=[VMEM] * (3 + len(pieces)),
        out_specs=VMEM,
        compiler_params=params(32),
        name="close",
    )(infos[side], tiles[side], sums, *[piece for piece, _, _ in pieces])


def project_body(quarters, last, base, w_in, w_out, *refs):
    parts, out = refs[:-1], refs[-1]
    rep = lax.axis_index("rep")
    core = lax.rem(lax.axis_index("dom"), 2)
    total = base[...]
    for part, (far, other) in zip(parts, quarters):
        width = part.shape[2]
        quarter = 2 * (1 - rep if far else rep) + (1 - core if other else core)
        span = pl.ds(pl.multiple_of(quarter * width, width), width)
        total = total + jnp.dot(part[0], w_in[span, :], preferred_element_type=F32)
        total = total + jnp.dot(part[1], w_out[span, :], preferred_element_type=F32)
    out[...] = jnp.maximum(total, 0.0).astype(BF16) if last else total


def project(base, parts, quarters, w_in, w_out, last):
    return pl.pallas_call(
        functools.partial(project_body, quarters, last),
        out_shape=jax.ShapeDtypeStruct(base.shape, BF16 if last else F32),
        in_specs=[VMEM] * (3 + len(parts)),
        out_specs=VMEM,
        compiler_params=params(24),
        cost_estimate=pl.CostEstimate(
            flops=len(parts) * 2**28, bytes_accessed=0, transcendentals=0
        ),
        name="project",
    )(base, w_in, w_out, *parts)


def on_device(features, tiles, columns, counts, degrees, w_self, w_in, w_out):
    devices = lax.axis_size("dom")
    reps = lax.axis_size("rep")
    width = features.shape[1] // (2 * reps)
    chips = devices // 2
    cores = core_route(devices)
    ahead, behind = ring_route(devices, 1), ring_route(devices, -1)

    mine, theirs, tiles, info = pack(features, tiles, columns, counts, degrees, width, devices)

    forward = [mine, theirs]
    backward = [mine, theirs]
    steps = []
    for step in range(1, (chips - 1) // 2 + 1):
        found = []
        for other in range(2):
            swap = other == 1 and step == 1
            forward[other] = lax.ppermute(forward[other], "dom", swapped(ahead) if swap else ahead)
            backward[other] = lax.ppermute(backward[other], "dom", swapped(behind) if swap else behind)
            found += [(forward[other], -step, other), (backward[other], step, other)]
        steps.append(found)
    last = [
        (lax.ppermute(forward[0], "dom", ahead), chips // 2, 0),
        (lax.ppermute(backward[1], "dom", behind), chips // 2, 1),
    ]
    sibling = lax.ppermute(theirs, "dom", cores)
    plan = (
        (info, lax.ppermute(info, "dom", cores)),
        (tiles, lax.ppermute(tiles, "dom", cores)),
    )
    early = [(mine, 0, 0), (sibling, 0, 1)] + [piece for found in steps[:-1] for piece in found]
    sums = absorb(plan, early, None, devices)
    sums = absorb(plan, steps[-1], sums, devices)
    other = close(plan, last, sums, 1, devices)
    own = close(plan, last, sums, 0, devices)

    across = [
        (d * reps + r, (d ^ 1) * reps + (r + 1) % reps) for d in range(devices) for r in range(reps)
    ]
    diagonal = lax.ppermute(other, ("dom", "rep"), across)
    core_side = lax.ppermute(other, "dom", cores)
    twin = lax.ppermute(own, "rep", [(r, (r + 1) % reps) for r in range(reps)])

    hidden = jnp.dot(features, w_self, preferred_element_type=F32)
    hidden = project(hidden, (own, core_side), ((0, 0), (0, 1)), w_in, w_out, False)
    hidden = project(hidden, (diagonal,), ((1, 1),), w_in, w_out, False)
    return project(hidden, (twin,), ((1, 0),), w_in, w_out, True)


def solution(mesh):
    placed = (
        P("dom", None),
        P(None, "dom", None, None, None),
        P(None, "dom", None),
        P(None, "dom"),
        P(None, "dom"),
        P(),
        P(),
        P(),
    )
    return jax.shard_map(
        on_device, mesh=mesh, in_specs=placed, out_specs=P("dom", None), check_vma=False
    )
```

```python
import functools

import jax
import jax.numpy as jnp
from jax import lax
from jax.experimental import pallas as pl
from jax.experimental.pallas import tpu as pltpu
from jax.sharding import PartitionSpec as P

F32 = jnp.float32
BF16 = jnp.bfloat16
SMEM = pl.BlockSpec(memory_space=pltpu.SMEM)
VMEM = pl.BlockSpec(memory_space=pltpu.VMEM)
HBM = pl.BlockSpec(memory_space=pltpu.HBM)


def params(mib):
    return pltpu.CompilerParams(vmem_limit_bytes=mib * 2**20)


def chip_ring(chips):
    half = chips // 2
    return [2 * o for o in range(half)] + [2 * o + 1 for o in reversed(range(half))]


def ring_route(devices, distance):
    ring = chip_ring(devices // 2)
    size = len(ring)
    route = []
    for place, chip in enumerate(ring):
        target = ring[(place + distance) % size]
        route += [(2 * chip + core, 2 * target + core) for core in range(2)]
    return sorted(route)


def swapped(route):
    return [(source, target ^ 1) for source, target in route]


def core_route(devices):
    return [(d, d ^ 1) for d in range(devices)]


def split(value, size):
    if size & (size - 1) == 0:
        return value >> (size.bit_length() - 1), value & (size - 1)
    return value // size, lax.rem(value, size)


def place_of(chip, chips):
    rung, side = split(chip, 2)
    return jnp.where(side == 0, rung, chips - 1 - rung)


def lane(offset, other, block, local):
    return (offset * 2 + other) * local + block


def pack_body(chips, local, features, bands, tiles, columns_in, counts_in, degrees_in, *refs):
    mine, theirs, bundle, columns, counts, degrees, arrived = refs
    rep = lax.axis_index("rep")
    position = lax.axis_index("dom")
    core = lax.rem(position, 2)
    here = place_of(position // 2, chips)
    width = mine.shape[1]
    tile = tiles.shape[1]
    slots = columns.shape[2]

    def quarter(core_of, start, size):
        return pl.ds(pl.multiple_of((2 * rep + core_of) * width + start, tile), size)

    moves = [
        (columns_in, columns),
        (counts_in, counts),
        (degrees_in, degrees),
        (features.at[:, quarter(core, 0, width)], mine),
        (features.at[:, quarter(1 - core, 0, width)], theirs),
        (tiles, bundle.at[0 : tiles.shape[0]]),
    ]
    index = tiles.shape[0]
    for start in range(0, width, tile):
        panel = bands.at[:, :, quarter(1 - core, start, tile)]
        moves.append((panel, bundle.at[index : index + bands.shape[0]]))
        index += bands.shape[0]
    copies = [
        pltpu.make_async_copy(source, target, arrived.at[number])
        for number, (source, target) in enumerate(moves)
    ]
    for copy in copies:
        copy.start()
    for copy in copies[:3]:
        copy.wait()
    column = jnp.concatenate([columns[relation] for relation in range(2)], axis=0)
    live = jnp.concatenate(
        [counts[relation : relation + 1, row : row + 1] for relation in range(2) for row in range(local)],
        axis=0,
    )
    source, block = split(column, local)
    chip, other = split(source, 2)
    _, offset = split(place_of(chip, chips) - here + chips, chips)
    other = jnp.where(core == 0, other, 1 - other)
    target = lane(offset, other, block, local)
    target = jnp.where(lax.broadcasted_iota(jnp.int32, column.shape, 1) < live, target, -1)
    place = lax.broadcasted_iota(jnp.int32, (2 * local, tile), 1)
    table = jnp.full(place.shape, -1, jnp.int32)
    for slot in range(slots):
        table = jnp.where(place == target[:, slot : slot + 1], slot, table)
    table = [table]
    for relation in range(2):
        for row in range(local):
            table.append(degrees[relation : relation + 1, row * tile : (row + 1) * tile])
    table = jnp.concatenate(table, axis=0).astype(F32)
    bundle[index, 0 : table.shape[0], :] = table.astype(BF16)
    for copy in copies[3:]:
        copy.wait()


def pack(features, tiles, columns, counts, degrees, width, devices):
    rows = features.shape[0]
    _, local, slots, tile, _ = tiles.shape
    assert devices * local <= tile
    panels = (rows // tile) * (width // tile)
    piece = jax.ShapeDtypeStruct((rows, width), BF16)
    bundle = jax.ShapeDtypeStruct((2 * local * slots + panels + 1, tile, tile), BF16)
    operands = [
        pltpu.with_memory_space_constraint(x, pltpu.HBM)
        for x in (
            features,
            features.reshape(rows // tile, tile, features.shape[1]),
            tiles.reshape(2 * local * slots, tile, tile),
            columns,
            counts,
            degrees,
        )
    ]
    return pl.pallas_call(
        functools.partial(pack_body, devices // 2, local),
        out_shape=[piece, piece, bundle],
        in_specs=[HBM] * 6,
        out_specs=[VMEM] * 3,
        scratch_shapes=[
            pltpu.VMEM(columns.shape, jnp.int32),
            pltpu.VMEM(counts.shape, jnp.int32),
            pltpu.VMEM(degrees.shape, jnp.int32),
            pltpu.SemaphoreType.DMA((6 + width // tile,)),
        ],
        compiler_params=params(24),
        name="pack",
    )(*operands)


def table_of(bundle):
    return bundle[bundle.shape[0] - 1, 0:8, :].astype(F32)


def packed_panel(bundle, rows, width):
    tile = bundle.shape[-1]
    across, count = width // tile, rows // tile
    first = bundle.shape[0] - 1 - count * across
    bands = []
    for band in range(count):
        parts = [bundle[first + part * count + band] for part in range(across)]
        bands.append(jnp.concatenate(parts, axis=1))
    return jnp.concatenate(bands, axis=0)


def contribution(table, bundle, local, slots, relation, row, side, panels, origins, chips):
    index = relation * local + row
    total = None
    for panel, (offset, other) in zip(panels, origins):
        weights = []
        for block in range(local):
            slot = table[index, lane(offset % chips, other ^ side, block, local)]
            one = bundle[index * slots + jnp.maximum(slot, 0)]
            weights.append(jnp.where(slot >= 0, one, jnp.zeros_like(one)))
        part = jnp.dot(
            jnp.concatenate(weights, axis=1), panel[...], preferred_element_type=F32
        )
        total = part if total is None else total + part
    return total


def absorb_body(origins, local, slots, chips, seeded, *refs):
    bundles = refs[:2]
    pieces, sums = list(refs[2:-1]), refs[-1]
    seed = pieces.pop() if seeded else None
    rows, width = sums.shape[2:]
    if not seeded:
        pieces.append(packed_panel(bundles[1], rows, width))
    tile = bundles[0].shape[-1]
    for side in range(2):
        table = table_of(bundles[side]).astype(jnp.int32)
        for relation in range(2):
            for row in range(local):
                span = slice(row * tile, (row + 1) * tile)
                part = contribution(
                    table, bundles[side], local, slots, relation, row, side, pieces, origins, chips
                )
                if seeded:
                    part = part + seed[side, relation, span, :]
                sums[side, relation, span, :] = part


def absorb(bundles, shape, pieces, sums, chips):
    local, slots = shape
    rows, width = pieces[0][0].shape
    origins = tuple((offset, other) for _, offset, other in pieces)
    seeds = [] if sums is None else [sums]
    if sums is None:
        origins += ((0, 1),)
    return pl.pallas_call(
        functools.partial(absorb_body, origins, local, slots, chips, sums is not None),
        out_shape=jax.ShapeDtypeStruct((2, 2, rows, width), F32),
        in_specs=[VMEM] * (2 + len(pieces) + len(seeds)),
        out_specs=VMEM,
        compiler_params=params(32),
        cost_estimate=pl.CostEstimate(
            flops=len(pieces) * 8 * rows * rows * width, bytes_accessed=0, transcendentals=0
        ),
        name="absorb",
    )(*bundles, *[piece for piece, _, _ in pieces], *seeds)


def close_body(origins, local, slots, chips, side, bundle, sums, *refs):
    pieces, outs = refs[: len(origins)], refs[len(origins) :]
    band_rows = outs[0].shape[1]
    tile = bundle.shape[-1]
    values = table_of(bundle)
    table = values.astype(jnp.int32)
    for relation in range(2):
        for row in range(local):
            span = slice(row * tile, (row + 1) * tile)
            total = sums[side, relation, span, :]
            total = total + contribution(
                table, bundle, local, slots, relation, row, side, pieces, origins, chips
            )
            index = 2 * local + relation * local + row
            degree = jnp.broadcast_to(values[index : index + 1, :], (tile, tile)).T
            for start in range(0, total.shape[1], tile):
                part = total[:, start : start + tile] / degree
                first = row * tile % band_rows
                out = outs[row * tile // band_rows]
                out[relation, first : first + tile, start : start + tile] = part.astype(BF16)


def close(bundle, shape, pieces, sums, side, chips, bands):
    local, slots = shape
    _, _, rows, width = sums.shape
    origins = tuple((offset, other) for _, offset, other in pieces)
    return pl.pallas_call(
        functools.partial(close_body, origins, local, slots, chips, side),
        out_shape=[jax.ShapeDtypeStruct((2, rows // bands, width), BF16)] * bands,
        in_specs=[VMEM] * (2 + len(pieces)),
        out_specs=[VMEM] * bands,
        compiler_params=params(32),
        name="close",
    )(bundle, sums, *[piece for piece, _, _ in pieces])


def project_body(quarters, bands, base, w_in, w_out, *refs):
    parts, out = list(refs[:-1]), refs[-1]
    rep = lax.axis_index("rep")
    core = lax.rem(lax.axis_index("dom"), 2)
    total = base[...]
    for (far, other), count in zip(quarters, bands):
        part, parts = parts[:count], parts[count:]
        width = part[0].shape[2]
        quarter = 2 * (1 - rep if far else rep) + (1 - core if other else core)
        span = pl.ds(pl.multiple_of(quarter * width, width), width)
        for relation, weights in enumerate((w_in, w_out)):
            rows = jnp.concatenate([band[relation] for band in part], axis=0)
            total = total + jnp.dot(rows, weights[span, :], preferred_element_type=F32)
    out[...] = total


def project(base, parts, quarters, w_in, w_out):
    bands = tuple(len(part) for part in parts)
    flat = [band for part in parts for band in part]
    return pl.pallas_call(
        functools.partial(project_body, quarters, bands),
        out_shape=jax.ShapeDtypeStruct(base.shape, F32),
        in_specs=[VMEM] * (3 + len(flat)),
        out_specs=VMEM,
        compiler_params=params(24),
        cost_estimate=pl.CostEstimate(
            flops=len(parts) * 2**28, bytes_accessed=0, transcendentals=0
        ),
        name="project",
    )(base, w_in, w_out, *flat)


def finish_body(band, quarter, base, w_in, w_out, part, *refs):
    out, staged, sent = refs[-3:]
    far, other = quarter
    rep = lax.axis_index("rep")
    core = lax.rem(lax.axis_index("dom"), 2)
    rows, width = part.shape[1:]
    quarter = 2 * (1 - rep if far else rep) + (1 - core if other else core)
    span = pl.ds(pl.multiple_of(quarter * width, width), width)
    first = band * rows
    total = base[first : first + rows, :]
    total = total + jnp.dot(part[0], w_in[span, :], preferred_element_type=F32)
    total = total + jnp.dot(part[1], w_out[span, :], preferred_element_type=F32)
    staged[...] = jnp.maximum(total, 0.0).astype(BF16)
    copy = pltpu.make_async_copy(staged, out.at[first : first + rows, :], sent)
    copy.start()
    copy.wait()


def finish(base, part, quarter, w_in, w_out, band, out):
    rows = part.shape[1]
    earlier = [] if out is None else [out]
    return pl.pallas_call(
        functools.partial(finish_body, band, quarter),
        out_shape=jax.ShapeDtypeStruct(base.shape, BF16),
        in_specs=[VMEM] * 4 + [HBM] * len(earlier),
        out_specs=HBM,
        scratch_shapes=[pltpu.VMEM((rows, base.shape[1]), BF16), pltpu.SemaphoreType.DMA],
        input_output_aliases={4: 0} if earlier else {},
        compiler_params=params(24),
        cost_estimate=pl.CostEstimate(flops=2**27, bytes_accessed=0, transcendentals=0),
        name="finish",
    )(base, w_in, w_out, part, *earlier)


def on_device(features, tiles, columns, counts, degrees, w_self, w_in, w_out):
    devices = lax.axis_size("dom")
    reps = lax.axis_size("rep")
    width = features.shape[1] // (2 * reps)
    chips = devices // 2
    cores = core_route(devices)
    ahead, behind = ring_route(devices, 1), ring_route(devices, -1)

    mine, theirs, bundle = pack(features, tiles, columns, counts, degrees, width, devices)
    bundles = (bundle, lax.ppermute(bundle, "dom", cores))
    shape = tiles.shape[1:3]

    forward = [mine, theirs]
    backward = [mine, theirs]
    steps = []
    for step in range(1, (chips - 1) // 2 + 1):
        found = []
        forward[1] = lax.ppermute(forward[1], "dom", swapped(ahead) if step == 1 else ahead)
        found.append((forward[1], -step, 1))
        backward[1] = lax.ppermute(backward[1], "dom", swapped(behind) if step == 1 else behind)
        found.append((backward[1], step, 1))
        forward[0] = lax.ppermute(forward[0], "dom", ahead)
        found.append((forward[0], -step, 0))
        backward[0] = lax.ppermute(backward[0], "dom", behind)
        found.append((backward[0], step, 0))
        steps.append(found)
    last = [
        (lax.ppermute(forward[1], "dom", ahead), chips // 2, 1),
        (lax.ppermute(backward[0], "dom", behind), chips // 2, 0),
    ]
    early = [(mine, 0, 0)] + [piece for found in steps[:-1] for piece in found]
    sums = absorb(bundles, shape, early, None, chips)
    sums = absorb(bundles, shape, steps[-1], sums, chips)
    (other,) = close(bundles[1], shape, last, sums, 1, chips, 1)
    owns = close(bundles[0], shape, last, sums, 0, chips, shape[0])

    across = [
        (d * reps + r, (d ^ 1) * reps + (r + 1) % reps) for d in range(devices) for r in range(reps)
    ]
    diagonal = lax.ppermute(other, ("dom", "rep"), across)
    core_side = lax.ppermute(other, "dom", cores)
    facing = [(r, (r + 1) % reps) for r in range(reps)]
    twins = [lax.ppermute(half, "rep", facing) for half in owns]

    hidden = jnp.dot(features, w_self, preferred_element_type=F32)
    hidden = project(hidden, [owns, [core_side]], ((0, 0), (0, 1)), w_in, w_out)
    hidden = project(hidden, [[diagonal]], ((1, 1),), w_in, w_out)
    out = None
    for band, twin in enumerate(twins):
        out = finish(hidden, twin, (1, 0), w_in, w_out, band, out)
    return out


def solution(mesh):
    placed = (
        P("dom", None),
        P(None, "dom", None, None, None),
        P(None, "dom", None),
        P(None, "dom"),
        P(None, "dom"),
        P(),
        P(),
        P(),
    )
    return jax.shard_map(
        on_device, mesh=mesh, in_specs=placed, out_specs=P("dom", None), check_vma=False
    )
```

```python
import functools

import jax
import jax.numpy as jnp
from jax import lax
from jax.experimental import pallas as pl
from jax.experimental.pallas import tpu as pltpu
from jax.sharding import PartitionSpec as P

F32 = jnp.float32
BF16 = jnp.bfloat16
SMEM = pl.BlockSpec(memory_space=pltpu.SMEM)
VMEM = pl.BlockSpec(memory_space=pltpu.VMEM)
HBM = pl.BlockSpec(memory_space=pltpu.HBM)


def params(mib):
    return pltpu.CompilerParams(vmem_limit_bytes=mib * 2**20)


def chip_ring(chips):
    half = chips // 2
    return [2 * o for o in range(half)] + [2 * o + 1 for o in reversed(range(half))]


def ring_route(devices, distance):
    ring = chip_ring(devices // 2)
    size = len(ring)
    route = []
    for place, chip in enumerate(ring):
        target = ring[(place + distance) % size]
        route += [(2 * chip + core, 2 * target + core) for core in range(2)]
    return sorted(route)


def swapped(route):
    return [(source, target ^ 1) for source, target in route]


def core_route(devices):
    return [(d, d ^ 1) for d in range(devices)]


def split(value, size):
    if size & (size - 1) == 0:
        return value >> (size.bit_length() - 1), value & (size - 1)
    return value // size, lax.rem(value, size)


def place_of(chip, chips):
    rung, side = split(chip, 2)
    return jnp.where(side == 0, rung, chips - 1 - rung)


def lane(offset, other, block, local):
    return (offset * 2 + other) * local + block


def pack_body(chips, local, features, bands, tiles, columns_in, counts_in, degrees_in, *refs):
    mine, theirs, bundle, columns, counts, degrees, arrived = refs
    rep = lax.axis_index("rep")
    position = lax.axis_index("dom")
    core = lax.rem(position, 2)
    here = place_of(position // 2, chips)
    width = mine.shape[1]
    tile = tiles.shape[1]
    slots = columns.shape[2]

    def quarter(core_of, start, size):
        return pl.ds(pl.multiple_of((2 * rep + core_of) * width + start, tile), size)

    moves = [
        (columns_in, columns),
        (counts_in, counts),
        (degrees_in, degrees),
        (features.at[:, quarter(core, 0, width)], mine),
        (features.at[:, quarter(1 - core, 0, width)], theirs),
        (tiles, bundle.at[0 : tiles.shape[0]]),
    ]
    index = tiles.shape[0]
    for start in range(0, width, tile):
        panel = bands.at[:, :, quarter(1 - core, start, tile)]
        moves.append((panel, bundle.at[index : index + bands.shape[0]]))
        index += bands.shape[0]
    copies = [
        pltpu.make_async_copy(source, target, arrived.at[number])
        for number, (source, target) in enumerate(moves)
    ]
    for copy in copies:
        copy.start()
    for copy in copies[:3]:
        copy.wait()
    column = jnp.concatenate([columns[relation] for relation in range(2)], axis=0)
    live = jnp.concatenate(
        [counts[relation : relation + 1, row : row + 1] for relation in range(2) for row in range(local)],
        axis=0,
    )
    source, block = split(column, local)
    chip, other = split(source, 2)
    _, offset = split(place_of(chip, chips) - here + chips, chips)
    other = jnp.where(core == 0, other, 1 - other)
    target = lane(offset, other, block, local)
    target = jnp.where(lax.broadcasted_iota(jnp.int32, column.shape, 1) < live, target, -1)
    place = lax.broadcasted_iota(jnp.int32, (2 * local, tile), 1)
    table = jnp.full(place.shape, -1, jnp.int32)
    for slot in range(slots):
        table = jnp.where(place == target[:, slot : slot + 1], slot, table)
    table = [table]
    for relation in range(2):
        for row in range(local):
            table.append(degrees[relation : relation + 1, row * tile : (row + 1) * tile])
    table = jnp.concatenate(table, axis=0).astype(F32)
    bundle[index, 0 : table.shape[0], :] = table.astype(BF16)
    for copy in copies[3:]:
        copy.wait()


def pack(features, tiles, columns, counts, degrees, width, devices):
    rows = features.shape[0]
    _, local, slots, tile, _ = tiles.shape
    assert devices * local <= tile
    panels = (rows // tile) * (width // tile)
    piece = jax.ShapeDtypeStruct((rows, width), BF16)
    bundle = jax.ShapeDtypeStruct((2 * local * slots + panels + 1, tile, tile), BF16)
    operands = [
        pltpu.with_memory_space_constraint(x, pltpu.HBM)
        for x in (
            features,
            features.reshape(rows // tile, tile, features.shape[1]),
            tiles.reshape(2 * local * slots, tile, tile),
            columns,
            counts,
            degrees,
        )
    ]
    return pl.pallas_call(
        functools.partial(pack_body, devices // 2, local),
        out_shape=[piece, piece, bundle],
        in_specs=[HBM] * 6,
        out_specs=[VMEM] * 3,
        scratch_shapes=[
            pltpu.VMEM(columns.shape, jnp.int32),
            pltpu.VMEM(counts.shape, jnp.int32),
            pltpu.VMEM(degrees.shape, jnp.int32),
            pltpu.SemaphoreType.DMA((6 + width // tile,)),
        ],
        compiler_params=params(24),
        name="pack",
    )(*operands)


def table_of(bundle):
    return bundle[bundle.shape[0] - 1, 0:8, :].astype(F32)


def packed_panel(bundle, rows, width):
    tile = bundle.shape[-1]
    across, count = width // tile, rows // tile
    first = bundle.shape[0] - 1 - count * across
    bands = []
    for band in range(count):
        parts = [bundle[first + part * count + band] for part in range(across)]
        bands.append(jnp.concatenate(parts, axis=1))
    return jnp.concatenate(bands, axis=0)


def contribution(table, bundle, local, slots, relation, row, side, panels, origins, chips):
    index = relation * local + row
    total = None
    for panel, (offset, other) in zip(panels, origins):
        weights = []
        for block in range(local):
            slot = table[index, lane(offset % chips, other ^ side, block, local)]
            one = bundle[index * slots + jnp.maximum(slot, 0)]
            weights.append(jnp.where(slot >= 0, one, jnp.zeros_like(one)))
        part = jnp.dot(
            jnp.concatenate(weights, axis=1), panel[...], preferred_element_type=F32
        )
        total = part if total is None else total + part
    return total


def absorb_body(origins, local, slots, chips, seeded, *refs):
    bundles = refs[:2]
    pieces, sums = list(refs[2:-1]), refs[-1]
    seed = pieces.pop() if seeded else None
    rows, width = sums.shape[2:]
    if not seeded:
        pieces.append(packed_panel(bundles[1], rows, width))
    tile = bundles[0].shape[-1]
    for side in range(2):
        table = table_of(bundles[side]).astype(jnp.int32)
        for relation in range(2):
            for row in range(local):
                span = slice(row * tile, (row + 1) * tile)
                part = contribution(
                    table, bundles[side], local, slots, relation, row, side, pieces, origins, chips
                )
                if seeded:
                    part = part + seed[side, relation, span, :]
                sums[side, relation, span, :] = part


def absorb(bundles, shape, pieces, sums, chips):
    local, slots = shape
    rows, width = pieces[0][0].shape
    origins = tuple((offset, other) for _, offset, other in pieces)
    seeds = [] if sums is None else [sums]
    if sums is None:
        origins += ((0, 1),)
    return pl.pallas_call(
        functools.partial(absorb_body, origins, local, slots, chips, sums is not None),
        out_shape=jax.ShapeDtypeStruct((2, 2, rows, width), F32),
        in_specs=[VMEM] * (2 + len(pieces) + len(seeds)),
        out_specs=VMEM,
        compiler_params=params(32),
        cost_estimate=pl.CostEstimate(
            flops=len(pieces) * 8 * rows * rows * width, bytes_accessed=0, transcendentals=0
        ),
        name="absorb",
    )(*bundles, *[piece for piece, _, _ in pieces], *seeds)


def close_body(origins, local, slots, chips, side, bundle, sums, *refs):
    pieces, outs = refs[: len(origins)], refs[len(origins) :]
    band_rows = outs[0].shape[1]
    tile = bundle.shape[-1]
    values = table_of(bundle)
    table = values.astype(jnp.int32)
    for relation in range(2):
        for row in range(local):
            span = slice(row * tile, (row + 1) * tile)
            total = sums[side, relation, span, :]
            total = total + contribution(
                table, bundle, local, slots, relation, row, side, pieces, origins, chips
            )
            index = 2 * local + relation * local + row
            degree = jnp.broadcast_to(values[index : index + 1, :], (tile, tile)).T
            for start in range(0, total.shape[1], tile):
                part = total[:, start : start + tile] / degree
                first = row * tile % band_rows
                out = outs[row * tile // band_rows]
                out[relation, first : first + tile, start : start + tile] = part.astype(BF16)


def close(bundle, shape, pieces, sums, side, chips, bands):
    local, slots = shape
    _, _, rows, width = sums.shape
    origins = tuple((offset, other) for _, offset, other in pieces)
    return pl.pallas_call(
        functools.partial(close_body, origins, local, slots, chips, side),
        out_shape=[jax.ShapeDtypeStruct((2, rows // bands, width), BF16)] * bands,
        in_specs=[VMEM] * (2 + len(pieces)),
        out_specs=[VMEM] * bands,
        compiler_params=params(32),
        name="close",
    )(bundle, sums, *[piece for piece, _, _ in pieces])


def project_body(quarters, bands, base, w_in, w_out, *refs):
    parts, out = list(refs[:-1]), refs[-1]
    rep = lax.axis_index("rep")
    core = lax.rem(lax.axis_index("dom"), 2)
    total = base[...]
    for (far, other), count in zip(quarters, bands):
        part, parts = parts[:count], parts[count:]
        width = part[0].shape[2]
        quarter = 2 * (1 - rep if far else rep) + (1 - core if other else core)
        span = pl.ds(pl.multiple_of(quarter * width, width), width)
        for relation, weights in enumerate((w_in, w_out)):
            rows = jnp.concatenate([band[relation] for band in part], axis=0)
            total = total + jnp.dot(rows, weights[span, :], preferred_element_type=F32)
    out[...] = total


def project(base, parts, quarters, w_in, w_out):
    bands = tuple(len(part) for part in parts)
    flat = [band for part in parts for band in part]
    return pl.pallas_call(
        functools.partial(project_body, quarters, bands),
        out_shape=jax.ShapeDtypeStruct(base.shape, F32),
        in_specs=[VMEM] * (3 + len(flat)),
        out_specs=VMEM,
        compiler_params=params(24),
        cost_estimate=pl.CostEstimate(
            flops=len(parts) * 2**28, bytes_accessed=0, transcendentals=0
        ),
        name="project",
    )(base, w_in, w_out, *flat)


def finish_body(band, quarter, base, w_in, w_out, part, *refs):
    out, staged, sent = refs[-3:]
    far, other = quarter
    rep = lax.axis_index("rep")
    core = lax.rem(lax.axis_index("dom"), 2)
    rows, width = part.shape[1:]
    quarter = 2 * (1 - rep if far else rep) + (1 - core if other else core)
    span = pl.ds(pl.multiple_of(quarter * width, width), width)
    first = band * rows
    total = base[first : first + rows, :]
    total = total + jnp.dot(part[0], w_in[span, :], preferred_element_type=F32)
    total = total + jnp.dot(part[1], w_out[span, :], preferred_element_type=F32)
    staged[...] = jnp.maximum(total, 0.0).astype(BF16)
    copy = pltpu.make_async_copy(staged, out.at[first : first + rows, :], sent)
    copy.start()
    copy.wait()


def finish(base, part, quarter, w_in, w_out, band, out):
    rows = part.shape[1]
    earlier = [] if out is None else [out]
    return pl.pallas_call(
        functools.partial(finish_body, band, quarter),
        out_shape=jax.ShapeDtypeStruct(base.shape, BF16),
        in_specs=[VMEM] * 4 + [HBM] * len(earlier),
        out_specs=HBM,
        scratch_shapes=[pltpu.VMEM((rows, base.shape[1]), BF16), pltpu.SemaphoreType.DMA],
        input_output_aliases={4: 0} if earlier else {},
        compiler_params=params(24),
        cost_estimate=pl.CostEstimate(flops=2**27, bytes_accessed=0, transcendentals=0),
        name="finish",
    )(base, w_in, w_out, part, *earlier)


def on_device(features, tiles, columns, counts, degrees, w_self, w_in, w_out):
    devices = lax.axis_size("dom")
    reps = lax.axis_size("rep")
    width = features.shape[1] // (2 * reps)
    chips = devices // 2
    cores = core_route(devices)
    ahead, behind = ring_route(devices, 1), ring_route(devices, -1)

    mine, theirs, bundle = pack(features, tiles, columns, counts, degrees, width, devices)
    bundles = (bundle, lax.ppermute(bundle, "dom", cores))
    shape = tiles.shape[1:3]

    forward = [mine, theirs]
    backward = [mine, theirs]
    steps = []
    for step in range(1, (chips - 1) // 2 + 1):
        found = []
        forward[1] = lax.ppermute(forward[1], "dom", swapped(ahead) if step == 1 else ahead)
        found.append((forward[1], -step, 1))
        backward[1] = lax.ppermute(backward[1], "dom", swapped(behind) if step == 1 else behind)
        found.append((backward[1], step, 1))
        forward[0] = lax.ppermute(forward[0], "dom", ahead)
        found.append((forward[0], -step, 0))
        backward[0] = lax.ppermute(backward[0], "dom", behind)
        found.append((backward[0], step, 0))
        steps.append(found)
    last = [
        (lax.ppermute(forward[1], "dom", ahead), chips // 2, 1),
        (lax.ppermute(backward[0], "dom", behind), chips // 2, 0),
    ]
    early = [(mine, 0, 0)] + [piece for found in steps[:-1] for piece in found]
    sums = absorb(bundles, shape, early, None, chips)
    sums = absorb(bundles, shape, steps[-1], sums, chips)
    (other,) = close(bundles[1], shape, last, sums, 1, chips, 1)
    owns = close(bundles[0], shape, last, sums, 0, chips, 1)

    facing = [(r, (r + 1) % reps) for r in range(reps)]
    passing = lax.ppermute(other, "rep", facing)
    twins = [lax.ppermute(half, "rep", facing) for half in owns]
    other, passing = lax.optimization_barrier((other, passing))
    core_side = lax.ppermute(other, "dom", cores)
    diagonal = lax.ppermute(passing, "dom", cores)

    hidden = jnp.dot(features, w_self, preferred_element_type=F32)
    hidden = project(hidden, [owns, [core_side]], ((0, 0), (0, 1)), w_in, w_out)
    hidden = project(hidden, [[diagonal]], ((1, 1),), w_in, w_out)
    out = None
    for band, twin in enumerate(twins):
        out = finish(hidden, twin, (1, 0), w_in, w_out, band, out)
    return out


def solution(mesh):
    placed = (
        P("dom", None),
        P(None, "dom", None, None, None),
        P(None, "dom", None),
        P(None, "dom"),
        P(None, "dom"),
        P(),
        P(),
        P(),
    )
    return jax.shard_map(
        on_device, mesh=mesh, in_specs=placed, out_specs=P("dom", None), check_vma=False
    )
```

```python
import functools

import jax
import jax.numpy as jnp
from jax import lax
from jax.experimental import pallas as pl
from jax.experimental.pallas import tpu as pltpu
from jax.sharding import PartitionSpec as P

F32 = jnp.float32
BF16 = jnp.bfloat16
SMEM = pl.BlockSpec(memory_space=pltpu.SMEM)
VMEM = pl.BlockSpec(memory_space=pltpu.VMEM)
HBM = pl.BlockSpec(memory_space=pltpu.HBM)


def params(mib):
    return pltpu.CompilerParams(vmem_limit_bytes=mib * 2**20)


def chip_ring(chips):
    half = chips // 2
    return [2 * o for o in range(half)] + [2 * o + 1 for o in reversed(range(half))]


def ring_route(devices, distance):
    ring = chip_ring(devices // 2)
    size = len(ring)
    route = []
    for place, chip in enumerate(ring):
        target = ring[(place + distance) % size]
        route += [(2 * chip + core, 2 * target + core) for core in range(2)]
    return sorted(route)


def swapped(route):
    return [(source, target ^ 1) for source, target in route]


def core_route(devices):
    return [(d, d ^ 1) for d in range(devices)]


def split(value, size):
    if size & (size - 1) == 0:
        return value >> (size.bit_length() - 1), value & (size - 1)
    return value // size, lax.rem(value, size)


def place_of(chip, chips):
    rung, side = split(chip, 2)
    return jnp.where(side == 0, rung, chips - 1 - rung)


def lane(offset, other, block, local):
    return (offset * 2 + other) * local + block


def pack_body(chips, local, features, bands, tiles, columns_in, counts_in, degrees_in, *refs):
    mine, theirs, bundle, columns, counts, degrees, arrived = refs
    rep = lax.axis_index("rep")
    position = lax.axis_index("dom")
    core = lax.rem(position, 2)
    here = place_of(position // 2, chips)
    width = mine.shape[1]
    tile = tiles.shape[1]
    slots = columns.shape[2]

    def quarter(core_of, start, size):
        return pl.ds(pl.multiple_of((2 * rep + core_of) * width + start, tile), size)

    moves = [
        (columns_in, columns),
        (counts_in, counts),
        (degrees_in, degrees),
        (features.at[:, quarter(core, 0, width)], mine),
        (features.at[:, quarter(1 - core, 0, width)], theirs),
        (tiles, bundle.at[0 : tiles.shape[0]]),
    ]
    index = tiles.shape[0]
    for start in range(0, width, tile):
        panel = bands.at[:, :, quarter(1 - core, start, tile)]
        moves.append((panel, bundle.at[index : index + bands.shape[0]]))
        index += bands.shape[0]
    copies = [
        pltpu.make_async_copy(source, target, arrived.at[number])
        for number, (source, target) in enumerate(moves)
    ]
    for copy in copies:
        copy.start()
    for copy in copies[:3]:
        copy.wait()
    column = jnp.concatenate([columns[relation] for relation in range(2)], axis=0)
    live = jnp.concatenate(
        [counts[relation : relation + 1, row : row + 1] for relation in range(2) for row in range(local)],
        axis=0,
    )
    source, block = split(column, local)
    chip, other = split(source, 2)
    _, offset = split(place_of(chip, chips) - here + chips, chips)
    other = jnp.where(core == 0, other, 1 - other)
    target = lane(offset, other, block, local)
    target = jnp.where(lax.broadcasted_iota(jnp.int32, column.shape, 1) < live, target, -1)
    place = lax.broadcasted_iota(jnp.int32, (2 * local, tile), 1)
    table = jnp.full(place.shape, -1, jnp.int32)
    for slot in range(slots):
        table = jnp.where(place == target[:, slot : slot + 1], slot, table)
    table = [table]
    for relation in range(2):
        for row in range(local):
            table.append(degrees[relation : relation + 1, row * tile : (row + 1) * tile])
    table = jnp.concatenate(table, axis=0).astype(F32)
    bundle[index, 0 : table.shape[0], :] = table.astype(BF16)
    for copy in copies[3:]:
        copy.wait()


def pack(features, tiles, columns, counts, degrees, width, devices):
    rows = features.shape[0]
    _, local, slots, tile, _ = tiles.shape
    assert devices * local <= tile
    panels = (rows // tile) * (width // tile)
    piece = jax.ShapeDtypeStruct((rows, width), BF16)
    bundle = jax.ShapeDtypeStruct((2 * local * slots + panels + 1, tile, tile), BF16)
    operands = [
        pltpu.with_memory_space_constraint(x, pltpu.HBM)
        for x in (
            features,
            features.reshape(rows // tile, tile, features.shape[1]),
            tiles.reshape(2 * local * slots, tile, tile),
            columns,
            counts,
            degrees,
        )
    ]
    return pl.pallas_call(
        functools.partial(pack_body, devices // 2, local),
        out_shape=[piece, piece, bundle],
        in_specs=[HBM] * 6,
        out_specs=[VMEM] * 3,
        scratch_shapes=[
            pltpu.VMEM(columns.shape, jnp.int32),
            pltpu.VMEM(counts.shape, jnp.int32),
            pltpu.VMEM(degrees.shape, jnp.int32),
            pltpu.SemaphoreType.DMA((6 + width // tile,)),
        ],
        compiler_params=params(24),
        name="pack",
    )(*operands)


def table_of(bundle):
    return bundle[bundle.shape[0] - 1, 0:8, :].astype(F32)


def packed_panel(bundle, rows, width):
    tile = bundle.shape[-1]
    across, count = width // tile, rows // tile
    first = bundle.shape[0] - 1 - count * across
    bands = []
    for band in range(count):
        parts = [bundle[first + part * count + band] for part in range(across)]
        bands.append(jnp.concatenate(parts, axis=1))
    return jnp.concatenate(bands, axis=0)


def contribution(table, bundle, local, slots, relation, row, side, panels, origins, chips):
    index = relation * local + row
    total = None
    for panel, (offset, other) in zip(panels, origins):
        weights = []
        for block in range(local):
            slot = table[index, lane(offset % chips, other ^ side, block, local)]
            one = bundle[index * slots + jnp.maximum(slot, 0)]
            weights.append(jnp.where(slot >= 0, one, jnp.zeros_like(one)))
        part = jnp.dot(
            jnp.concatenate(weights, axis=1), panel[...], preferred_element_type=F32
        )
        total = part if total is None else total + part
    return total


def absorb_body(origins, local, slots, chips, seeded, *refs):
    bundles = refs[:2]
    pieces, sums = list(refs[2:-1]), refs[-1]
    seed = pieces.pop() if seeded else None
    rows, width = sums.shape[2:]
    if not seeded:
        pieces.append(packed_panel(bundles[1], rows, width))
    tile = bundles[0].shape[-1]
    for side in range(2):
        table = table_of(bundles[side]).astype(jnp.int32)
        for relation in range(2):
            for row in range(local):
                span = slice(row * tile, (row + 1) * tile)
                part = contribution(
                    table, bundles[side], local, slots, relation, row, side, pieces, origins, chips
                )
                if seeded:
                    part = part + seed[side, relation, span, :]
                sums[side, relation, span, :] = part


def absorb(bundles, shape, pieces, sums, chips):
    local, slots = shape
    rows, width = pieces[0][0].shape
    origins = tuple((offset, other) for _, offset, other in pieces)
    seeds = [] if sums is None else [sums]
    if sums is None:
        origins += ((0, 1),)
    return pl.pallas_call(
        functools.partial(absorb_body, origins, local, slots, chips, sums is not None),
        out_shape=jax.ShapeDtypeStruct((2, 2, rows, width), F32),
        in_specs=[VMEM] * (2 + len(pieces) + len(seeds)),
        out_specs=VMEM,
        compiler_params=params(32),
        cost_estimate=pl.CostEstimate(
            flops=len(pieces) * 8 * rows * rows * width, bytes_accessed=0, transcendentals=0
        ),
        name="absorb",
    )(*bundles, *[piece for piece, _, _ in pieces], *seeds)


def close_body(origins, local, slots, chips, side, bundle, sums, *refs):
    pieces, outs = refs[: len(origins)], refs[len(origins) :]
    band_rows = outs[0].shape[1]
    tile = bundle.shape[-1]
    values = table_of(bundle)
    table = values.astype(jnp.int32)
    for relation in range(2):
        for row in range(local):
            span = slice(row * tile, (row + 1) * tile)
            total = sums[side, relation, span, :]
            total = total + contribution(
                table, bundle, local, slots, relation, row, side, pieces, origins, chips
            )
            index = 2 * local + relation * local + row
            degree = jnp.broadcast_to(values[index : index + 1, :], (tile, tile)).T
            for start in range(0, total.shape[1], tile):
                part = total[:, start : start + tile] / degree
                first = row * tile % band_rows
                out = outs[row * tile // band_rows]
                out[relation, first : first + tile, start : start + tile] = part.astype(BF16)


def close(bundle, shape, pieces, sums, side, chips, bands):
    local, slots = shape
    _, _, rows, width = sums.shape
    origins = tuple((offset, other) for _, offset, other in pieces)
    return pl.pallas_call(
        functools.partial(close_body, origins, local, slots, chips, side),
        out_shape=[jax.ShapeDtypeStruct((2, rows // bands, width), BF16)] * bands,
        in_specs=[VMEM] * (2 + len(pieces)),
        out_specs=[VMEM] * bands,
        compiler_params=params(32),
        name="close",
    )(bundle, sums, *[piece for piece, _, _ in pieces])


def project_body(quarters, bands, base, w_in, w_out, *refs):
    parts, out = list(refs[:-1]), refs[-1]
    rep = lax.axis_index("rep")
    core = lax.rem(lax.axis_index("dom"), 2)
    total = base[...]
    for (far, other), count in zip(quarters, bands):
        part, parts = parts[:count], parts[count:]
        width = part[0].shape[2]
        quarter = 2 * (1 - rep if far else rep) + (1 - core if other else core)
        span = pl.ds(pl.multiple_of(quarter * width, width), width)
        for relation, weights in enumerate((w_in, w_out)):
            rows = jnp.concatenate([band[relation] for band in part], axis=0)
            total = total + jnp.dot(rows, weights[span, :], preferred_element_type=F32)
    out[...] = total


def project(base, parts, quarters, w_in, w_out):
    bands = tuple(len(part) for part in parts)
    flat = [band for part in parts for band in part]
    return pl.pallas_call(
        functools.partial(project_body, quarters, bands),
        out_shape=jax.ShapeDtypeStruct(base.shape, F32),
        in_specs=[VMEM] * (3 + len(flat)),
        out_specs=VMEM,
        compiler_params=params(24),
        cost_estimate=pl.CostEstimate(
            flops=len(parts) * 2**28, bytes_accessed=0, transcendentals=0
        ),
        name="project",
    )(base, w_in, w_out, *flat)


def finish_body(band, quarter, base, w_in, w_out, part, *refs):
    out, staged, sent = refs[-3:]
    far, other = quarter
    rep = lax.axis_index("rep")
    core = lax.rem(lax.axis_index("dom"), 2)
    rows, width = part.shape[1:]
    quarter = 2 * (1 - rep if far else rep) + (1 - core if other else core)
    span = pl.ds(pl.multiple_of(quarter * width, width), width)
    first = band * rows
    total = base[first : first + rows, :]
    total = total + jnp.dot(part[0], w_in[span, :], preferred_element_type=F32)
    total = total + jnp.dot(part[1], w_out[span, :], preferred_element_type=F32)
    staged[...] = jnp.maximum(total, 0.0).astype(BF16)
    copy = pltpu.make_async_copy(staged, out.at[first : first + rows, :], sent)
    copy.start()
    copy.wait()


def finish(base, part, quarter, w_in, w_out, band, out):
    rows = part.shape[1]
    earlier = [] if out is None else [out]
    return pl.pallas_call(
        functools.partial(finish_body, band, quarter),
        out_shape=jax.ShapeDtypeStruct(base.shape, BF16),
        in_specs=[VMEM] * 4 + [HBM] * len(earlier),
        out_specs=HBM,
        scratch_shapes=[pltpu.VMEM((rows, base.shape[1]), BF16), pltpu.SemaphoreType.DMA],
        input_output_aliases={4: 0} if earlier else {},
        compiler_params=params(24),
        cost_estimate=pl.CostEstimate(flops=2**27, bytes_accessed=0, transcendentals=0),
        name="finish",
    )(base, w_in, w_out, part, *earlier)


def on_device(features, tiles, columns, counts, degrees, w_self, w_in, w_out):
    devices = lax.axis_size("dom")
    reps = lax.axis_size("rep")
    width = features.shape[1] // (2 * reps)
    chips = devices // 2
    cores = core_route(devices)
    ahead, behind = ring_route(devices, 1), ring_route(devices, -1)

    mine, theirs, bundle = pack(features, tiles, columns, counts, degrees, width, devices)
    bundles = (bundle, lax.ppermute(bundle, "dom", cores))
    shape = tiles.shape[1:3]

    forward = [mine, theirs]
    backward = [mine, theirs]
    steps = []
    for step in range(1, (chips - 1) // 2 + 1):
        found = []
        forward[1] = lax.ppermute(forward[1], "dom", swapped(ahead) if step == 1 else ahead)
        found.append((forward[1], -step, 1))
        backward[1] = lax.ppermute(backward[1], "dom", swapped(behind) if step == 1 else behind)
        found.append((backward[1], step, 1))
        forward[0] = lax.ppermute(forward[0], "dom", ahead)
        found.append((forward[0], -step, 0))
        backward[0] = lax.ppermute(backward[0], "dom", behind)
        found.append((backward[0], step, 0))
        steps.append(found)
    last = [
        (lax.ppermute(forward[1], "dom", ahead), chips // 2, 1),
        (lax.ppermute(backward[0], "dom", behind), chips // 2, 0),
    ]
    early = [(mine, 0, 0)] + [piece for found in steps for piece in found]
    sums = absorb(bundles, shape, early, None, chips)
    (other,) = close(bundles[1], shape, last, sums, 1, chips, 1)
    owns = close(bundles[0], shape, last, sums, 0, chips, 1)

    facing = [(r, (r + 1) % reps) for r in range(reps)]
    passing = lax.ppermute(other, "rep", facing)
    twins = [lax.ppermute(half, "rep", facing) for half in owns]
    other, passing = lax.optimization_barrier((other, passing))
    core_side = lax.ppermute(other, "dom", cores)
    diagonal = lax.ppermute(passing, "dom", cores)

    hidden = jnp.dot(features, w_self, preferred_element_type=F32)
    hidden = project(hidden, [owns], ((0, 0),), w_in, w_out)
    hidden = project(hidden, [[core_side], [diagonal]], ((0, 1), (1, 1)), w_in, w_out)
    out = None
    for band, twin in enumerate(twins):
        out = finish(hidden, twin, (1, 0), w_in, w_out, band, out)
    return out


def solution(mesh):
    placed = (
        P("dom", None),
        P(None, "dom", None, None, None),
        P(None, "dom", None),
        P(None, "dom"),
        P(None, "dom"),
        P(),
        P(),
        P(),
    )
    return jax.shard_map(
        on_device, mesh=mesh, in_specs=placed, out_specs=P("dom", None), check_vma=False
    )
```

```python
import functools

import jax
import jax.numpy as jnp
from jax import lax
from jax.experimental import pallas as pl
from jax.experimental.pallas import tpu as pltpu
from jax.sharding import PartitionSpec as P

F32 = jnp.float32
BF16 = jnp.bfloat16
SMEM = pl.BlockSpec(memory_space=pltpu.SMEM)
VMEM = pl.BlockSpec(memory_space=pltpu.VMEM)
HBM = pl.BlockSpec(memory_space=pltpu.HBM)


def params(mib):
    return pltpu.CompilerParams(vmem_limit_bytes=mib * 2**20)


def chip_ring(chips):
    half = chips // 2
    return [2 * o for o in range(half)] + [2 * o + 1 for o in reversed(range(half))]


def ring_route(devices, distance):
    ring = chip_ring(devices // 2)
    size = len(ring)
    route = []
    for place, chip in enumerate(ring):
        target = ring[(place + distance) % size]
        route += [(2 * chip + core, 2 * target + core) for core in range(2)]
    return sorted(route)


def swapped(route):
    return [(source, target ^ 1) for source, target in route]


def core_route(devices):
    return [(d, d ^ 1) for d in range(devices)]


def split(value, size):
    if size & (size - 1) == 0:
        return value >> (size.bit_length() - 1), value & (size - 1)
    return value // size, lax.rem(value, size)


def place_of(chip, chips):
    rung, side = split(chip, 2)
    return jnp.where(side == 0, rung, chips - 1 - rung)


def lane(offset, other, block, local):
    return (offset * 2 + other) * local + block


def pack_body(chips, local, features, bands, tiles, columns_in, counts_in, degrees_in, *refs):
    mine, theirs, bundle, columns, counts, degrees, arrived = refs
    rep = lax.axis_index("rep")
    position = lax.axis_index("dom")
    core = lax.rem(position, 2)
    here = place_of(position // 2, chips)
    width = mine.shape[1]
    tile = tiles.shape[1]
    slots = columns.shape[2]

    def quarter(core_of, start, size):
        return pl.ds(pl.multiple_of((2 * rep + core_of) * width + start, tile), size)

    moves = [
        (columns_in, columns),
        (counts_in, counts),
        (degrees_in, degrees),
        (features.at[:, quarter(core, 0, width)], mine),
        (features.at[:, quarter(1 - core, 0, width)], theirs),
        (tiles, bundle.at[0 : tiles.shape[0]]),
    ]
    index = tiles.shape[0]
    for start in range(0, width, tile):
        panel = bands.at[:, :, quarter(1 - core, start, tile)]
        moves.append((panel, bundle.at[index : index + bands.shape[0]]))
        index += bands.shape[0]
    copies = [
        pltpu.make_async_copy(source, target, arrived.at[number])
        for number, (source, target) in enumerate(moves)
    ]
    for copy in copies:
        copy.start()
    for copy in copies[:3]:
        copy.wait()
    column = jnp.concatenate([columns[relation] for relation in range(2)], axis=0)
    live = jnp.concatenate(
        [counts[relation : relation + 1, row : row + 1] for relation in range(2) for row in range(local)],
        axis=0,
    )
    source, block = split(column, local)
    chip, other = split(source, 2)
    _, offset = split(place_of(chip, chips) - here + chips, chips)
    other = jnp.where(core == 0, other, 1 - other)
    target = lane(offset, other, block, local)
    target = jnp.where(lax.broadcasted_iota(jnp.int32, column.shape, 1) < live, target, -1)
    place = lax.broadcasted_iota(jnp.int32, (2 * local, tile), 1)
    table = jnp.full(place.shape, -1, jnp.int32)
    for slot in range(slots):
        table = jnp.where(place == target[:, slot : slot + 1], slot, table)
    table = [table]
    for relation in range(2):
        for row in range(local):
            table.append(degrees[relation : relation + 1, row * tile : (row + 1) * tile])
    table = jnp.concatenate(table, axis=0).astype(F32)
    bundle[index, 0 : table.shape[0], :] = table.astype(BF16)
    for copy in copies[3:]:
        copy.wait()


def pack(features, tiles, columns, counts, degrees, width, devices):
    rows = features.shape[0]
    _, local, slots, tile, _ = tiles.shape
    assert devices * local <= tile
    panels = (rows // tile) * (width // tile)
    piece = jax.ShapeDtypeStruct((rows, width), BF16)
    bundle = jax.ShapeDtypeStruct((2 * local * slots + panels + 1, tile, tile), BF16)
    operands = [
        pltpu.with_memory_space_constraint(x, pltpu.HBM)
        for x in (
            features,
            features.reshape(rows // tile, tile, features.shape[1]),
            tiles.reshape(2 * local * slots, tile, tile),
            columns,
            counts,
            degrees,
        )
    ]
    return pl.pallas_call(
        functools.partial(pack_body, devices // 2, local),
        out_shape=[piece, piece, bundle],
        in_specs=[HBM] * 6,
        out_specs=[VMEM] * 3,
        scratch_shapes=[
            pltpu.VMEM(columns.shape, jnp.int32),
            pltpu.VMEM(counts.shape, jnp.int32),
            pltpu.VMEM(degrees.shape, jnp.int32),
            pltpu.SemaphoreType.DMA((6 + width // tile,)),
        ],
        compiler_params=params(24),
        name="pack",
    )(*operands)


def table_of(bundle):
    return bundle[bundle.shape[0] - 1, 0:8, :].astype(F32)


def packed_panel(bundle, rows, width):
    tile = bundle.shape[-1]
    across, count = width // tile, rows // tile
    first = bundle.shape[0] - 1 - count * across
    bands = []
    for band in range(count):
        parts = [bundle[first + part * count + band] for part in range(across)]
        bands.append(jnp.concatenate(parts, axis=1))
    return jnp.concatenate(bands, axis=0)


def contribution(table, bundle, local, slots, relation, row, side, panels, origins, chips):
    index = relation * local + row
    total = None
    for panel, (offset, other) in zip(panels, origins):
        weights = []
        for block in range(local):
            slot = table[index, lane(offset % chips, other ^ side, block, local)]
            one = bundle[index * slots + jnp.maximum(slot, 0)]
            weights.append(jnp.where(slot >= 0, one, jnp.zeros_like(one)))
        part = jnp.dot(
            jnp.concatenate(weights, axis=1), panel[...], preferred_element_type=F32
        )
        total = part if total is None else total + part
    return total


def absorb_body(origins, local, slots, chips, seeded, *refs):
    bundles = refs[:2]
    pieces, sums = list(refs[2:-1]), refs[-1]
    seed = pieces.pop() if seeded else None
    rows, width = sums.shape[2:]
    if not seeded:
        pieces.append(packed_panel(bundles[1], rows, width))
    tile = bundles[0].shape[-1]
    for side in range(2):
        table = table_of(bundles[side]).astype(jnp.int32)
        for relation in range(2):
            for row in range(local):
                span = slice(row * tile, (row + 1) * tile)
                part = contribution(
                    table, bundles[side], local, slots, relation, row, side, pieces, origins, chips
                )
                if seeded:
                    part = part + seed[side, relation, span, :]
                sums[side, relation, span, :] = part


def absorb(bundles, shape, pieces, sums, chips):
    local, slots = shape
    rows, width = pieces[0][0].shape
    origins = tuple((offset, other) for _, offset, other in pieces)
    seeds = [] if sums is None else [sums]
    if sums is None:
        origins += ((0, 1),)
    return pl.pallas_call(
        functools.partial(absorb_body, origins, local, slots, chips, sums is not None),
        out_shape=jax.ShapeDtypeStruct((2, 2, rows, width), F32),
        in_specs=[VMEM] * (2 + len(pieces) + len(seeds)),
        out_specs=VMEM,
        compiler_params=params(32),
        cost_estimate=pl.CostEstimate(
            flops=len(pieces) * 8 * rows * rows * width, bytes_accessed=0, transcendentals=0
        ),
        name="absorb",
    )(*bundles, *[piece for piece, _, _ in pieces], *seeds)


def close_body(origins, local, slots, chips, side, bundle, sums, *refs):
    pieces, outs = refs[: len(origins)], refs[len(origins) :]
    band_rows = outs[0].shape[1]
    tile = bundle.shape[-1]
    values = table_of(bundle)
    table = values.astype(jnp.int32)
    for relation in range(2):
        for row in range(local):
            span = slice(row * tile, (row + 1) * tile)
            total = sums[side, relation, span, :]
            total = total + contribution(
                table, bundle, local, slots, relation, row, side, pieces, origins, chips
            )
            index = 2 * local + relation * local + row
            degree = jnp.broadcast_to(values[index : index + 1, :], (tile, tile)).T
            for start in range(0, total.shape[1], tile):
                part = total[:, start : start + tile] / degree
                first = row * tile % band_rows
                out = outs[row * tile // band_rows]
                out[relation, first : first + tile, start : start + tile] = part.astype(BF16)


def close(bundle, shape, pieces, sums, side, chips, bands):
    local, slots = shape
    _, _, rows, width = sums.shape
    origins = tuple((offset, other) for _, offset, other in pieces)
    return pl.pallas_call(
        functools.partial(close_body, origins, local, slots, chips, side),
        out_shape=[jax.ShapeDtypeStruct((2, rows // bands, width), BF16)] * bands,
        in_specs=[VMEM] * (2 + len(pieces)),
        out_specs=[VMEM] * bands,
        compiler_params=params(32),
        name="close",
    )(bundle, sums, *[piece for piece, _, _ in pieces])


def project_body(quarters, bands, base, w_in, w_out, *refs):
    parts, out = list(refs[:-1]), refs[-1]
    rep = lax.axis_index("rep")
    core = lax.rem(lax.axis_index("dom"), 2)
    total = base[...]
    for (far, other), count in zip(quarters, bands):
        part, parts = parts[:count], parts[count:]
        width = part[0].shape[2]
        quarter = 2 * (1 - rep if far else rep) + (1 - core if other else core)
        span = pl.ds(pl.multiple_of(quarter * width, width), width)
        for relation, weights in enumerate((w_in, w_out)):
            rows = jnp.concatenate([band[relation] for band in part], axis=0)
            total = total + jnp.dot(rows, weights[span, :], preferred_element_type=F32)
    out[...] = total


def project(base, parts, quarters, w_in, w_out):
    bands = tuple(len(part) for part in parts)
    flat = [band for part in parts for band in part]
    return pl.pallas_call(
        functools.partial(project_body, quarters, bands),
        out_shape=jax.ShapeDtypeStruct(base.shape, F32),
        in_specs=[VMEM] * (3 + len(flat)),
        out_specs=VMEM,
        compiler_params=params(24),
        cost_estimate=pl.CostEstimate(
            flops=len(parts) * 2**28, bytes_accessed=0, transcendentals=0
        ),
        name="project",
    )(base, w_in, w_out, *flat)


def finish_body(band, quarter, base, w_in, w_out, part, *refs):
    out, staged, sent = refs[-3:]
    far, other = quarter
    rep = lax.axis_index("rep")
    core = lax.rem(lax.axis_index("dom"), 2)
    rows, width = part.shape[1:]
    quarter = 2 * (1 - rep if far else rep) + (1 - core if other else core)
    span = pl.ds(pl.multiple_of(quarter * width, width), width)
    first = band * rows
    total = base[first : first + rows, :]
    total = total + jnp.dot(part[0], w_in[span, :], preferred_element_type=F32)
    total = total + jnp.dot(part[1], w_out[span, :], preferred_element_type=F32)
    staged[...] = jnp.maximum(total, 0.0).astype(BF16)
    copy = pltpu.make_async_copy(staged, out.at[first : first + rows, :], sent)
    copy.start()
    copy.wait()


def finish(base, part, quarter, w_in, w_out, band, out):
    rows = part.shape[1]
    earlier = [] if out is None else [out]
    return pl.pallas_call(
        functools.partial(finish_body, band, quarter),
        out_shape=jax.ShapeDtypeStruct(base.shape, BF16),
        in_specs=[VMEM] * 4 + [HBM] * len(earlier),
        out_specs=HBM,
        scratch_shapes=[pltpu.VMEM((rows, base.shape[1]), BF16), pltpu.SemaphoreType.DMA],
        input_output_aliases={4: 0} if earlier else {},
        compiler_params=params(24),
        cost_estimate=pl.CostEstimate(flops=2**27, bytes_accessed=0, transcendentals=0),
        name="finish",
    )(base, w_in, w_out, part, *earlier)


def on_device(features, tiles, columns, counts, degrees, w_self, w_in, w_out):
    devices = lax.axis_size("dom")
    reps = lax.axis_size("rep")
    width = features.shape[1] // (2 * reps)
    chips = devices // 2
    cores = core_route(devices)
    ahead, behind = ring_route(devices, 1), ring_route(devices, -1)

    mine, theirs, bundle = pack(features, tiles, columns, counts, degrees, width, devices)
    bundles = (bundle, lax.ppermute(bundle, "dom", cores))
    shape = tiles.shape[1:3]

    forward = [mine, theirs]
    backward = [mine, theirs]
    steps = []
    for step in range(1, (chips - 1) // 2 + 1):
        found = []
        forward[0] = lax.ppermute(forward[0], "dom", ahead)
        found.append((forward[0], -step, 0))
        backward[0] = lax.ppermute(backward[0], "dom", behind)
        found.append((backward[0], step, 0))
        forward[1] = lax.ppermute(forward[1], "dom", swapped(ahead) if step == 1 else ahead)
        found.append((forward[1], -step, 1))
        backward[1] = lax.ppermute(backward[1], "dom", swapped(behind) if step == 1 else behind)
        found.append((backward[1], step, 1))
        steps.append(found)
    last = [
        (lax.ppermute(forward[0], "dom", ahead), chips // 2, 0),
        (lax.ppermute(backward[1], "dom", behind), chips // 2, 1),
    ]
    early = [(mine, 0, 0)] + [piece for found in steps for piece in found]
    sums = absorb(bundles, shape, early, None, chips)
    (other,) = close(bundles[1], shape, last, sums, 1, chips, 1)
    owns = close(bundles[0], shape, last, sums, 0, chips, 1)

    facing = [(r, (r + 1) % reps) for r in range(reps)]
    passing = lax.ppermute(other, "rep", facing)
    twins = [lax.ppermute(half, "rep", facing) for half in owns]
    other, passing = lax.optimization_barrier((other, passing))
    core_side = lax.ppermute(other, "dom", cores)
    diagonal = lax.ppermute(passing, "dom", cores)

    hidden = jnp.dot(features, w_self, preferred_element_type=F32)
    hidden = project(hidden, [owns], ((0, 0),), w_in, w_out)
    hidden = project(hidden, [[core_side], [diagonal]], ((0, 1), (1, 1)), w_in, w_out)
    out = None
    for band, twin in enumerate(twins):
        out = finish(hidden, twin, (1, 0), w_in, w_out, band, out)
    return out


def solution(mesh):
    placed = (
        P("dom", None),
        P(None, "dom", None, None, None),
        P(None, "dom", None),
        P(None, "dom"),
        P(None, "dom"),
        P(),
        P(),
        P(),
    )
    return jax.shard_map(
        on_device, mesh=mesh, in_specs=placed, out_specs=P("dom", None), check_vma=False
    )
```
